32 devices in a mesh: ctx: 4 (over z), head: 4 (over y, x), seg: 2 (over core).
Axes of the slice: x: 2, y: 2, z: 4, core: 2. Of those that a mesh axis runs over, the one named last changes fastest.
Arguments:
- tokens_x: bfloat16 [4096, 2560], P(('ctx', 'seg'), 'head'), may hold values from -6 to 6
- gate_weight: bfloat16 [64, 3, 2560], P(None, None, 'head'), may hold values from -0.15625 to 0.15625
- queries: bfloat16 [4096, 64, 192], P(('ctx', 'seg'), 'head'), may hold values from -48 to 48
- keys: bfloat16 [4096, 4, 192], P(('ctx', 'seg'), 'head'), may hold values from -7 to 7
- values: bfloat16 [4096, 4, 128], P(('ctx', 'seg'), 'head'), may hold values from -24 to 24
- comp_key_weight: bfloat16 [4, 32, 192], P('head'), may hold values from -1 to 1
- comp_value_weight: bfloat16 [4, 32, 128], P('head'), may hold values from -1 to 1
- selected: int32 [32, 4, 16], P(('ctx', 'seg'), 'head'), may hold values from -1 to 63, as said below
Outputs:
- attention: bfloat16 [4096, 64, 128], P(('ctx', 'seg'), 'head')
The draws below stay inside these ranges and needn't reach their ends.
Inputs may be any that keep to these rules, and one draw needn't show every extreme that they name: Each list names the tile's own fine blocks and block 0, then further blocks; live entries are distinct and at most the tile's last fine block; -1 marks an empty entry. For the tiles of one device (one block of 512 tokens) and one group, the blocks selected from the segment of 512 tokens of any other device number at most 1, and some device reaches it.
All inputs are finite; a program needn't handle non-finite values.
Results may differ from the reference program's by a relative error of at most 0.0059.
Values may be sent and summed in bfloat16 or wider, within the bound.
A program may use at most 128 MiB of HBM per device.

```python
import jax
import jax.numpy as jnp
from jax import lax

D = 2560
H = 64
G = 4
DK = 192
DV = 128
TILE = 128
BLK_S = 64
BLK_C = 32
NSEL = 16
WINDOW = 512
PEER_CAP = 1
TOK_DEV = 512
TOKENS = 4096


def draw_pair(key):
    query_key = jax.random.fold_in(key, 11)
    key_key = jax.random.fold_in(key, 12)
    keys_out = jnp.clip(jax.random.normal(key_key, (TOKENS, G, DK), jnp.float32), -6.0, 6.0)
    queries_out = jnp.clip(jax.random.normal(query_key, (TOKENS, H, DK), jnp.float32), -6.0, 6.0)
    return (queries_out, keys_out)


def draw_queries(key, part):
    return draw_pair(key)[0].astype(jnp.bfloat16)


def draw_keys(key, part):
    return draw_pair(key)[1].astype(jnp.bfloat16)


def draw_selected(key, part):
    block_count = TOKENS // BLK_S
    per_device = TOK_DEV // BLK_S
    device_count = TOKENS // TOK_DEV
    tile_count = TOKENS // TILE
    tile_blocks = TILE // BLK_S
    owner_key = jax.random.fold_in(key, 21)
    score_key = jax.random.fold_in(key, 22)
    block_ids = jnp.arange(block_count, dtype=jnp.int32)
    picks = jax.random.randint(owner_key, (device_count, G, block_count), 0, 2 ** 12) * per_device + block_ids % per_device
    picks = jnp.where(block_ids == 0, 2 ** 30, picks)
    grouped = picks.reshape(device_count, G, device_count, per_device)
    beaten = jnp.sum((grouped[..., None, :] > grouped[..., :, None]).astype(jnp.int32), axis=-1)
    marked = (beaten < PEER_CAP).reshape(device_count, G, block_count)
    tiles = jnp.arange(tile_count, dtype=jnp.int32)
    device_of = tiles // (TOK_DEV // TILE)
    marked_tile = marked[device_of]
    last = ((tiles + 1) * tile_blocks - 1)[:, None, None]
    first = (tiles * tile_blocks)[:, None, None]
    owner = (block_ids // per_device)[None, None, :]
    device_b = device_of[:, None, None]
    causal = block_ids[None, None, :] <= last
    candidate = causal & ((owner == device_b) | marked_tile)
    random_part = jax.random.randint(score_key, (tile_count, G, block_count), 0, 2 ** 12)
    distance = jnp.maximum(last - block_ids[None, None, :], 0)
    base = jnp.where(owner == device_b, random_part * 64 // (distance + 4), random_part * 16)
    score = jnp.where(block_ids[None, None, :] >= first, 2 ** 30, jnp.where(block_ids[None, None, :] == 0, 2 ** 29, jnp.where((owner == device_b - 1) & marked_tile, 2 ** 28, base * block_count)))
    score = jnp.where(candidate, score + block_ids[None, None, :], -1 - block_ids[None, None, :])
    top_values, top_index = lax.top_k(score, NSEL)
    return jnp.where(top_values >= 0, top_index, -1).astype(jnp.int32)


def strengthened(drawn, own_key, source, target, parts, factor):
    def block_of(dim):
        return (jnp.arange(drawn.shape[dim]) // (drawn.shape[dim] // parts)).reshape((-1,) + (1,) * (drawn.ndim - 1 - dim))

    one_side = jax.random.permutation(own_key, parts)[block_of(target)]
    far = (block_of(target) + parts // 2) % parts
    return jnp.where((block_of(source) == one_side) | (block_of(source) == far), factor * drawn, drawn)


def levels(key, extent, split, least, top_value):
    def one(dim, blocks):
        heights = jax.random.uniform(jax.random.fold_in(jax.random.fold_in(key, 6), dim), (blocks,), jnp.float32, least / len(split), top_value / len(split))
        return jnp.repeat(jnp.exp(heights), extent[dim] // blocks).reshape((-1,) + (1,) * (len(extent) - dim - 1))

    loudness = one(*split[0])
    for cut in split[1:]:
        loudness = loudness * one(*cut)
    return loudness


def gaussian(own_key, shape, spread, most, shards=(), kind=jnp.bfloat16):
    result = spread * jax.random.normal(own_key, shape, jnp.float32)
    if shards:
        result = result * levels(own_key, shape, shards, -0.22, 0.18)
    return jnp.clip(result, -most, most).astype(kind)


def bell_draw_with(own_key, dims, scale, reach, shards, heavy, held_as=jnp.bfloat16):
    entries = scale * jax.random.normal(own_key, dims, jnp.float32)
    if shards:
        entries = entries * levels(own_key, dims, shards, -0.22, 0.18)
    return jnp.clip(strengthened(entries, jax.random.fold_in(own_key, 3), *heavy), -reach, reach).astype(held_as)


def setup_inputs(seed: int = 0) -> dict:
    arg_keys = jax.random.split(jax.random.key(seed), 9)
    tokens_x = gaussian(arg_keys[0], (TOKENS, D), 1.0, 6.0, ((0, 8), (1, 4)))
    gate_weight = bell_draw_with(arg_keys[1], (H, 3, D), D ** -0.5, 0.15625, ((2, 4),), (2, 0, 4, 2.0))
    queries = draw_queries(jax.random.fold_in(arg_keys[8], 71), 0)
    keys = draw_keys(jax.random.fold_in(arg_keys[8], 71), 0)
    values = gaussian(arg_keys[4], (TOKENS, G, DV), 4.0, 24.0, ((0, 8), (1, 4)))
    comp_key_weight = gaussian(arg_keys[5], (G, BLK_C, DK), BLK_C ** -0.5, 1.0, ((0, 4),))
    comp_value_weight = gaussian(arg_keys[6], (G, BLK_C, DV), BLK_C ** -0.5, 1.0, ((0, 4),))
    selected = draw_selected(jax.random.fold_in(arg_keys[8], 71), 0)
    return {"tokens_x": tokens_x, "gate_weight": gate_weight, "queries": queries, "keys": keys, "values": values, "comp_key_weight": comp_key_weight, "comp_value_weight": comp_value_weight, "selected": selected}


def attend(query, keys_part, values_part, allowed):
    scores = jnp.einsum('rhd,kd->hrk', query.astype(jnp.float32), keys_part.astype(jnp.float32)) * (keys_part.shape[-1] ** -0.5)
    scores = jnp.where(allowed[None], scores, -1e30)
    highest = jnp.max(scores, axis=-1, keepdims=True)
    weights = jnp.where(allowed[None], jnp.exp(scores - highest), 0.0)
    total = jnp.sum(weights, axis=-1)
    rounded = lax.optimization_barrier(weights.astype(jnp.bfloat16))
    summed = jnp.einsum('hrk,kv->rhv', rounded.astype(jnp.float32), values_part.astype(jnp.float32))
    return summed / jnp.maximum(total, 1.0).T[:, :, None]


def reference(tokens_x, gate_weight, queries, keys, values, comp_key_weight, comp_value_weight, selected):
    group_heads = H // G
    logits = jnp.einsum('hcd,td->hct', gate_weight.astype(jnp.float32), tokens_x.astype(jnp.float32))
    gates = jax.nn.sigmoid(logits)
    coarse_count = TOKENS // BLK_C
    key_blocks = keys.astype(jnp.float32).reshape(coarse_count, BLK_C, G, DK)
    value_blocks = values.astype(jnp.float32).reshape(coarse_count, BLK_C, G, DV)
    coarse_keys = jnp.sum(key_blocks * jnp.transpose(comp_key_weight.astype(jnp.float32), (1, 0, 2))[None], axis=1).astype(jnp.bfloat16)
    coarse_values = jnp.sum(value_blocks * jnp.transpose(comp_value_weight.astype(jnp.float32), (1, 0, 2))[None], axis=1).astype(jnp.bfloat16)
    coarse_end = jnp.arange(coarse_count, dtype=jnp.int32) * BLK_C + BLK_C - 1
    padded_keys = jnp.pad(keys, ((WINDOW, 0), (0, 0), (0, 0)))
    padded_values = jnp.pad(values, ((WINDOW, 0), (0, 0), (0, 0)))
    fine_keys_all = keys.reshape(TOKENS // BLK_S, BLK_S, G, DK)
    fine_values_all = values.reshape(TOKENS // BLK_S, BLK_S, G, DV)

    def one_tile(tile):
        start = (tile * TILE).astype(jnp.int32)
        rows = start + jnp.arange(TILE, dtype=jnp.int32)
        query = lax.dynamic_slice_in_dim(queries, start, TILE, 0)
        gate = lax.dynamic_slice_in_dim(gates, start, TILE, 2)
        near_keys = lax.dynamic_slice_in_dim(padded_keys, start, WINDOW + TILE, 0)
        near_values = lax.dynamic_slice_in_dim(padded_values, start, WINDOW + TILE, 0)
        near_pos = start - WINDOW + jnp.arange(WINDOW + TILE, dtype=jnp.int32)
        near_ok = (near_pos[None, :] >= 0) & (near_pos[None, :] <= rows[:, None]) & (near_pos[None, :] > rows[:, None] - WINDOW)
        coarse_ok = coarse_end[None, :] <= rows[:, None]
        chosen = selected[tile]
        outputs = []
        for group in range(G):
            blocks = jnp.maximum(chosen[group], 0)
            fine_keys = fine_keys_all[blocks, :, group].reshape(NSEL * BLK_S, DK)
            fine_values = fine_values_all[blocks, :, group].reshape(NSEL * BLK_S, DV)
            fine_pos = (blocks[:, None] * BLK_S + jnp.arange(BLK_S, dtype=jnp.int32)[None, :]).reshape(-1)
            live = jnp.repeat(chosen[group] >= 0, BLK_S)
            fine_ok = live[None, :] & (fine_pos[None, :] <= rows[:, None])
            head_query = query[:, group * group_heads:(group + 1) * group_heads]
            head_gate = gate[group * group_heads:(group + 1) * group_heads]
            coarse_out = attend(head_query, coarse_keys[:, group], coarse_values[:, group], coarse_ok)
            fine_out = attend(head_query, fine_keys, fine_values, fine_ok)
            window_out = attend(head_query, near_keys[:, group], near_values[:, group], near_ok)
            mixed = head_gate[:, 0, :].T[:, :, None] * coarse_out + head_gate[:, 1, :].T[:, :, None] * fine_out
            mixed = mixed + head_gate[:, 2, :].T[:, :, None] * window_out
            outputs.append(mixed)
        return jnp.concatenate(outputs, axis=1).astype(jnp.bfloat16)

    tiles = lax.map(one_tile, jnp.arange(TOKENS // TILE, dtype=jnp.int32))
    return tiles.reshape(TOKENS, H, DV)
```

```python
import functools

import jax
import jax.numpy as jnp
from jax import lax
from jax.experimental import pallas as pl
from jax.experimental.pallas import tpu as pltpu
from jax.sharding import PartitionSpec as P

TILE = 128
BLK_S = 64
BLK_C = 32
NSEL = 16
WINDOW = 512
HEADS = 4
BOUND = 40.0

MESH = pl.DeviceIdType.MESH
NT = (((1,), (1,)), ((), ()))
NN = (((1,), (0,)), ((), ()))


def dot(a, b, dims=NN):
    return lax.dot_general(a, b, dims, preferred_element_type=jnp.float32)


def exchange_kernel(
    n, segs, heads,
    x_ref, w_ref, kt_ref, v_ref, cwk_ref, cwv_ref, sel_ref,
    g_ref, pk_ref, pv_ref, ck_ref, cv_ref, bk_ref, bv_ref,
    part, got, cks, cvs, sels, stk, stv, ssem, rsem, gs, gr,
):
    local = v_ref.shape[0]
    coarse = local // BLK_C
    share = g_ref.shape[0]
    ctx, seg, head = lax.axis_index("ctx"), lax.axis_index("seg"), lax.axis_index("head")
    me = ctx * segs + seg

    def ring(steps):
        other = lax.rem(me + steps + n, n)
        return {"ctx": other // segs, "seg": lax.rem(other, segs)}

    def peer(steps):
        return {"head": lax.rem(head + steps + heads, heads)}

    barrier = pltpu.get_barrier_semaphore()
    for r in range(1, n):
        pl.semaphore_signal(barrier, inc=1, device_id=ring(r), device_id_type=MESH)
    for r in range(1, heads):
        pl.semaphore_signal(barrier, inc=1, device_id=peer(r), device_id_type=MESH)

    cks[...] = jnp.sum(
        kt_ref[...].astype(jnp.float32).T.reshape(coarse, BLK_C, -1)
        * cwk_ref[...].astype(jnp.float32)[None], axis=1
    ).astype(jnp.bfloat16)
    cvs[...] = jnp.sum(
        v_ref[...].astype(jnp.float32).reshape(coarse, BLK_C, -1)
        * cwv_ref[...].astype(jnp.float32)[None], axis=1
    ).astype(jnp.bfloat16)

    pl.semaphore_wait(barrier, n - 1 + heads - 1)

    def send(src, dst, kind, slot, where):
        copy = pltpu.make_async_remote_copy(
            src_ref=src, dst_ref=dst, send_sem=ssem.at[kind, slot],
            recv_sem=rsem.at[kind, slot], device_id=where, device_id_type=MESH,
        )
        copy.start()
        return copy

    lists = [send(sel_ref, sels.at[r - 1], 0, r - 1, ring(-r)) for r in range(1, n)]
    rest = [send(kt_ref, pk_ref, 5, 0, ring(1)), send(v_ref, pv_ref, 5, 1, ring(1))]

    gates = dot(w_ref[...], x_ref[...], NT)
    hc = share // 3
    for h in range(heads):
        for c in range(3):
            first = (c * heads + h) * hc
            part[h, c * hc:(c + 1) * hc] = gates[first:first + hc]

    mine = pl.ds(pl.multiple_of(me * coarse, coarse), coarse)
    for r in range(1, n):
        rest.append(send(cks, ck_ref.at[mine], 1, r - 1, ring(r)))
        rest.append(send(cvs, cv_ref.at[mine], 2, r - 1, ring(r)))
    ck_ref[mine, :] = cks[...]
    cv_ref[mine, :] = cvs[...]
    sums = []
    for r in range(1, heads):
        copy = pltpu.make_async_remote_copy(
            src_ref=part.at[lax.rem(head + r, heads)], dst_ref=got.at[r - 1],
            send_sem=gs.at[r - 1], recv_sem=gr.at[r - 1],
            device_id=peer(r), device_id_type=MESH,
        )
        copy.start()
        sums.append(copy)

    per = local // BLK_S
    for r in range(1, n):
        lists[r - 1].wait()
        asked = sels[r - 1]
        hit = (asked >= me * per) & (asked < (me + 1) * per)
        want = jnp.where(hit, asked - me * per, 0)
        want = jnp.max(jnp.max(want, axis=1, keepdims=True), axis=0, keepdims=True)
        ahead = lax.broadcasted_iota(jnp.int32, (BLK_S, local), 1) - lax.broadcasted_iota(
            jnp.int32, (BLK_S, local), 0
        )
        pick = jnp.where(ahead == want * BLK_S, 1.0, 0.0).astype(jnp.bfloat16)
        stk[r - 1] = dot(pick, kt_ref[...], NT).astype(jnp.bfloat16)
        stv[r - 1] = dot(pick, v_ref[...]).astype(jnp.bfloat16)
    bk_ref[(n - 1) * BLK_S:, :] = jnp.zeros((BLK_S, bk_ref.shape[1]), jnp.bfloat16)
    bv_ref[(n - 1) * BLK_S:, :] = jnp.zeros((BLK_S, bv_ref.shape[1]), jnp.bfloat16)
    for r in range(1, n):
        rows = pl.ds((r - 1) * BLK_S, BLK_S)
        rest.append(send(stk.at[r - 1], bk_ref.at[rows], 3, r - 1, ring(r)))
        rest.append(send(stv.at[r - 1], bv_ref.at[rows], 4, r - 1, ring(r)))

    for copy in sums:
        copy.wait()
    total = part[head]
    for r in range(1, heads):
        total = total + got[r - 1]
    g_ref[...] = jax.nn.sigmoid(total)
    for copy in rest:
        copy.wait()


def attention_kernel(
    n, segs, hc, local,
    sel_ref, q_ref, kt_ref, v_ref, pk_ref, pv_ref, bk_ref, bv_ref, ck_ref, cv_ref, g_ref,
    o_ref,
    kw, vtw, vtp, lw, lp, lc, mixed_ref, knorm,
):
    f32, bf16 = jnp.float32, jnp.bfloat16
    me = lax.axis_index("ctx") * segs + lax.axis_index("seg")
    tile = pl.program_id(0)
    sub = pl.program_id(1)
    rows = TILE * HEADS
    span = WINDOW + TILE
    dk = kt_ref.shape[0]
    dv = v_ref.shape[1]
    nc = ck_ref.shape[0]
    npk = (n - 1) * BLK_S
    per = local // BLK_S
    coef = dk ** -0.5

    @pl.when((tile == 0) & (sub == 0))
    def _():
        kw[:WINDOW] = pk_ref[:, local - WINDOW:].astype(f32).T.astype(bf16)
        kw[WINDOW:] = kt_ref[...].astype(f32).T.astype(bf16)
        vtw[:, :WINDOW] = pv_ref[local - WINDOW:, :].astype(f32).T.astype(bf16)
        vtw[:, WINDOW:] = v_ref[...].astype(f32).T.astype(bf16)
        vtp[...] = bv_ref[...].astype(f32).T.astype(bf16)
        lc[:dv] = cv_ref[...].astype(f32).T.astype(bf16)
        lc[dv:] = jnp.where(
            lax.broadcasted_iota(jnp.int32, (16, nc), 0) == 0, 1.0, 0.0
        ).astype(bf16)
        top = jnp.zeros((1, 1), f32)
        for ref in (kw, bk_ref, ck_ref):
            part = ref[...].astype(f32)
            top = jnp.maximum(top, jnp.max(jnp.sum(part * part, axis=1, keepdims=True), axis=0, keepdims=True))
        knorm[0] = jnp.max(top)

    def chosen(blocks, keep):
        found = jnp.zeros(blocks.shape, jnp.bool_)
        for i in range(NSEL):
            found = found | (blocks == sel_ref[tile, i])
        return found & keep

    def chosen_peer(owner):
        found = jnp.zeros(owner.shape, jnp.bool_)
        for i in range(NSEL):
            entry = sel_ref[tile, i]
            found = found | ((owner * per <= entry) & (entry < owner * per + per))
        return found & (owner >= 0)

    def window_parts(shape, dim):
        pos = me * local + tile * TILE - WINDOW + lax.broadcasted_iota(jnp.int32, shape, dim)
        own = chosen(pos // BLK_S, pos >= me * local)
        return pos >= 0, own

    def peer_part(shape, dim):
        slot = lax.broadcasted_iota(jnp.int32, shape, dim) // BLK_S
        return chosen_peer(me - 1 - slot)

    @pl.when(sub == 0)
    def _():
        valid, own = window_parts((1, span), 1)
        valid, own = valid.astype(f32), own.astype(f32)
        begin = pl.multiple_of(tile * TILE, TILE)
        vt = vtw[:, pl.ds(begin, span)].astype(f32)
        lw[:dv] = (vt * valid).astype(bf16)
        lw[dv:2 * dv] = (vt * own).astype(bf16)
        line = lax.broadcasted_iota(jnp.int32, (16, span), 0)
        lw[2 * dv:] = jnp.where(line == 0, valid, jnp.where(line == 1, own, 0.0)).astype(bf16)
        live = peer_part((1, npk), 1).astype(f32)
        lp[:dv] = (vtp[:, :npk].astype(f32) * live).astype(bf16)
        line = lax.broadcasted_iota(jnp.int32, (16, npk), 0)
        lp[dv:] = jnp.where(line == 0, live, 0.0).astype(bf16)

    q = jnp.concatenate([q_ref[h] for h in range(HEADS)], axis=1)

    def gate(c):
        first = c * hc + sub * HEADS
        return jnp.concatenate([g_ref[pl.ds(first + h, 1), :] for h in range(HEADS)], axis=1)

    gate_c, gate_f, gate_w = gate(0), gate(1), gate(2)
    begin = pl.multiple_of(tile * TILE, TILE)
    keys_w = kw[pl.ds(begin, span), :]
    keys_p = bk_ref[:npk, :]
    square = q.astype(f32)
    qn = dot(jnp.ones((8, dk), bf16), (square * square).astype(bf16))
    safe = jnp.max(qn) * knorm[0] * (1.02 * coef * coef) < BOUND * BOUND

    def token(shape):
        return lax.rem(lax.broadcasted_iota(jnp.int32, shape, 1), TILE)

    def coarse_mask():
        shape = (nc, rows)
        end = lax.broadcasted_iota(jnp.int32, shape, 0) * BLK_C + (BLK_C - 1)
        return end <= token(shape) + (me * local + tile * TILE)

    def put(mixed):
        for h in range(HEADS):
            mixed_ref[pl.ds(sub * HEADS + h, TILE, stride=hc), :] = mixed[:, h * TILE:(h + 1) * TILE].T

    @pl.when(safe)
    def _():
        scale = coef * 1.4426950408889634
        ew = jnp.exp2(dot(keys_w, q) * scale)
        key = lax.broadcasted_iota(jnp.int32, (TILE, rows), 0)
        tok = token((TILE, rows))
        low = jnp.where(key > tok, ew[:TILE], 0.0)
        high = jnp.where(key <= tok, ew[WINDOW:], 0.0)
        ew = jnp.concatenate(
            [low.astype(bf16), ew[TILE:WINDOW].astype(bf16), high.astype(bf16)], axis=0
        )
        ow = dot(lw[...], ew)
        ep = jnp.exp2(dot(keys_p, q) * scale).astype(bf16)
        op = dot(lp[...], ep)
        ec = jnp.exp2(dot(ck_ref[...], q) * scale)
        oc = dot(lc[...], jnp.where(coarse_mask(), ec, 0.0).astype(bf16))
        tw = ow[2 * dv:2 * dv + 1]
        tf = ow[2 * dv + 1:2 * dv + 2] + op[dv:dv + 1]
        tc = oc[dv:dv + 1]

        def share(gate, total):
            return jnp.where(total > 0.0, gate / jnp.where(total > 0.0, total, 1.0), 0.0)

        mixed = (
            share(gate_c, tc) * oc[:dv]
            + share(gate_f, tf) * (ow[dv:2 * dv] + op[:dv])
            + share(gate_w, tw) * ow[:dv]
        )
        put(mixed)

    @pl.when(jnp.logical_not(safe))
    def _():
        tok = token((span, rows))
        key = lax.broadcasted_iota(jnp.int32, (span, rows), 0)
        valid, own = window_parts((span, rows), 0)
        causal = key - WINDOW <= tok
        sw = dot(keys_w, q) * coef
        sp = dot(keys_p, q) * coef
        sc = dot(ck_ref[...], q) * coef

        def top(scores, allowed):
            return jnp.max(jnp.where(allowed, scores, -1e30), axis=0, keepdims=True)

        def weigh(scores, allowed, high):
            e = jnp.where(allowed, jnp.exp(jnp.where(allowed, scores - high, 0.0)), 0.0)
            return e.astype(bf16), jnp.sum(e, axis=0, keepdims=True)

        vt = vtw[:, pl.ds(begin, span)]
        ok = valid & causal & (key > tok)
        e, total = weigh(sw, ok, top(sw, ok))
        out_w = dot(vt, e) / jnp.maximum(total, 1.0)
        ok = own & causal
        live = peer_part((npk, rows), 0)
        high = jnp.maximum(top(sw, ok), top(sp, live))
        e, total = weigh(sw, ok, high)
        ep, more = weigh(sp, live, high)
        out_f = (dot(vt, e) + dot(vtp[:, :npk], ep)) / jnp.maximum(total + more, 1.0)
        ok = coarse_mask()
        e, total = weigh(sc, ok, top(sc, ok))
        out_c = dot(lc[:dv], e) / jnp.maximum(total, 1.0)
        mixed = gate_c * out_c + gate_f * out_f + gate_w * out_w
        put(mixed)

    @pl.when(sub == hc // HEADS - 1)
    def _():
        o_ref[...] = mixed_ref[...].astype(bf16)


def on_device(
    n, segs, heads,
    tokens_x, gate_weight, queries, keys, values, comp_key_weight, comp_value_weight, selected,
):
    bf16, f32 = jnp.bfloat16, jnp.float32
    local, hc, dk = queries.shape
    dv = values.shape[2]
    rows_w = gate_weight.shape[0] * gate_weight.shape[1]
    weight = jnp.transpose(gate_weight, (1, 0, 2)).reshape(rows_w, -1)
    share = rows_w // heads
    k2, v2 = keys.reshape(local, dk).T, values.reshape(local, dv)
    chosen = selected.reshape(selected.shape[0], NSEL)
    coarse = local // BLK_C
    vmem = pl.BlockSpec(memory_space=pltpu.VMEM)
    shape = jax.ShapeDtypeStruct
    gates, pk, pv, ck, cv, bk, bv = pl.pallas_call(
        functools.partial(exchange_kernel, n, segs, heads),
        out_shape=[
            shape((share, local), f32),
            shape((dk, local), bf16), shape((local, dv), bf16),
            shape((n * coarse, dk), bf16), shape((n * coarse, dv), bf16),
            shape((n * BLK_S, dk), bf16), shape((n * BLK_S, dv), bf16),
        ],
        in_specs=[vmem] * 7,
        out_specs=[vmem] * 7,
        scratch_shapes=[
            pltpu.VMEM((heads, share, local), f32),
            pltpu.VMEM((heads - 1, share, local), f32),
            pltpu.VMEM((coarse, dk), bf16),
            pltpu.VMEM((coarse, dv), bf16),
            pltpu.VMEM((n - 1,) + chosen.shape, jnp.int32),
            pltpu.VMEM((n - 1, BLK_S, dk), bf16),
            pltpu.VMEM((n - 1, BLK_S, dv), bf16),
            pltpu.SemaphoreType.DMA((6, n)),
            pltpu.SemaphoreType.DMA((6, n)),
            pltpu.SemaphoreType.DMA((heads,)),
            pltpu.SemaphoreType.DMA((heads,)),
        ],
        compiler_params=pltpu.CompilerParams(collective_id=0, has_side_effects=True),
        name="exchange",
    )(tokens_x, weight, k2, v2, comp_key_weight[0], comp_value_weight[0], chosen)

    rows = TILE * hc
    span = WINDOW + TILE
    npk = (n - 1) * BLK_S
    out = pl.pallas_call(
        functools.partial(attention_kernel, n, segs, hc, local),
        grid=(local // TILE, hc // HEADS),
        out_shape=shape((local * hc, dv), bf16),
        in_specs=[
            pl.BlockSpec(memory_space=pltpu.SMEM),
            pl.BlockSpec((HEADS, dk, TILE), lambda i, j: (j, 0, i)),
        ] + [vmem] * 8 + [pl.BlockSpec((share, TILE), lambda i, j: (0, i))],
        out_specs=pl.BlockSpec((rows, dv), lambda i, j: (i, 0)),
        scratch_shapes=[
            pltpu.VMEM((WINDOW + local, dk), bf16),
            pltpu.VMEM((dv, WINDOW + local), bf16),
            pltpu.VMEM((dv, n * BLK_S), bf16),
            pltpu.VMEM((2 * dv + 16, span), bf16),
            pltpu.VMEM((dv + 16, npk), bf16),
            pltpu.VMEM((dv + 16, n * coarse), bf16),
            pltpu.VMEM((rows, dv), f32),
            pltpu.SMEM((1,), f32),
        ],
        compiler_params=pltpu.CompilerParams(
            dimension_semantics=("arbitrary", "arbitrary"), vmem_limit_bytes=60 * 1024 * 1024
        ),
        name="attend",
    )(chosen, jnp.transpose(queries, (1, 2, 0)), k2, v2, pk, pv, bk, bv, ck, cv, gates)
    return out.reshape(local, hc, dv)


def solution(mesh):
    in_specs = (
        P(("ctx", "seg"), "head"),
        P(None, None, "head"),
        P(("ctx", "seg"), "head", None),
        P(("ctx", "seg"), "head", None),
        P(("ctx", "seg"), "head", None),
        P("head", None, None),
        P("head", None, None),
        P(("ctx", "seg"), "head", None),
    )
    n = mesh.shape["ctx"] * mesh.shape["seg"]
    return jax.shard_map(
        functools.partial(on_device, n, mesh.shape["seg"], mesh.shape["head"]),
        mesh=mesh, in_specs=in_specs, out_specs=P(("ctx", "seg"), "head", None), check_vma=False,
    )
```

```python
import functools

import jax
import jax.numpy as jnp
from jax import lax
from jax.experimental import pallas as pl
from jax.experimental.pallas import tpu as pltpu
from jax.sharding import PartitionSpec as P

TILE = 128
BLK_S = 64
BLK_C = 32
NSEL = 16
WINDOW = 512
KEY_ROWS = 1 << 22
BOUND = 40.0

MESH = pl.DeviceIdType.MESH
NT = (((1,), (1,)), ((), ()))
NN = (((1,), (0,)), ((), ()))


def dot(a, b, dims=NN):
    return lax.dot_general(a, b, dims, preferred_element_type=jnp.float32)


def exchange_kernel(
    n, segs, heads,
    x_ref, w_ref, kt_ref, v_ref, cwk_ref, cwv_ref, sel_ref, q_hbm,
    g_ref, pk_ref, pv_ref, ck_ref, cv_ref, bk_ref, bv_ref, qn_ref,
    part, got, cks, cvs, sels, stk, stv, qs, ssem, rsem, gs, gr, qsem,
):
    local = v_ref.shape[0]
    coarse = local // BLK_C
    share = g_ref.shape[0]
    ctx, seg, head = lax.axis_index("ctx"), lax.axis_index("seg"), lax.axis_index("head")
    me = ctx * segs + seg

    def ring(steps):
        other = lax.rem(me + steps + n, n)
        return {"ctx": other // segs, "seg": lax.rem(other, segs)}

    def peer(steps):
        return {"head": lax.rem(head + steps + heads, heads)}

    fetch = pltpu.make_async_copy(q_hbm, qs, qsem)
    fetch.start()
    barrier = pltpu.get_barrier_semaphore()
    for r in range(1, n):
        pl.semaphore_signal(barrier, inc=1, device_id=ring(r), device_id_type=MESH)
    for r in range(1, heads):
        pl.semaphore_signal(barrier, inc=1, device_id=peer(r), device_id_type=MESH)

    cks[...] = jnp.sum(
        kt_ref[...].astype(jnp.float32).T.reshape(coarse, BLK_C, -1)
        * cwk_ref[...].astype(jnp.float32)[None], axis=1
    ).astype(jnp.bfloat16)
    cvs[...] = jnp.sum(
        v_ref[...].astype(jnp.float32).reshape(coarse, BLK_C, -1)
        * cwv_ref[...].astype(jnp.float32)[None], axis=1
    ).astype(jnp.bfloat16)

    pl.semaphore_wait(barrier, n - 1 + heads - 1)

    def send(src, dst, kind, slot, where):
        copy = pltpu.make_async_remote_copy(
            src_ref=src, dst_ref=dst, send_sem=ssem.at[kind, slot],
            recv_sem=rsem.at[kind, slot], device_id=where, device_id_type=MESH,
        )
        copy.start()
        return copy

    lists = [send(sel_ref, sels.at[r - 1], 0, r - 1, ring(-r)) for r in range(1, n)]
    rest = [send(kt_ref, pk_ref, 5, 0, ring(1)), send(v_ref, pv_ref, 5, 1, ring(1))]

    gates = dot(w_ref[...], x_ref[...], NT)
    hc = share // 3
    for h in range(heads):
        for c in range(3):
            first = (c * heads + h) * hc
            part[h, c * hc:(c + 1) * hc] = gates[first:first + hc]

    mine = pl.ds(pl.multiple_of(me * coarse, coarse), coarse)
    for r in range(1, n):
        rest.append(send(cks, ck_ref.at[mine], 1, r - 1, ring(r)))
        rest.append(send(cvs, cv_ref.at[mine], 2, r - 1, ring(r)))
    ck_ref[mine, :] = cks[...]
    cv_ref[mine, :] = cvs[...]
    sums = []
    for r in range(1, heads):
        copy = pltpu.make_async_remote_copy(
            src_ref=part.at[lax.rem(head + r, heads)], dst_ref=got.at[r - 1],
            send_sem=gs.at[r - 1], recv_sem=gr.at[r - 1],
            device_id=peer(r), device_id_type=MESH,
        )
        copy.start()
        sums.append(copy)

    per = local // BLK_S
    for r in range(1, n):
        lists[r - 1].wait()
        asked = sels[r - 1]
        hit = (asked >= me * per) & (asked < (me + 1) * per)
        want = jnp.where(hit, asked - me * per, 0)
        want = jnp.max(jnp.max(want, axis=1, keepdims=True), axis=0, keepdims=True)
        ahead = lax.broadcasted_iota(jnp.int32, (BLK_S, local), 1) - lax.broadcasted_iota(
            jnp.int32, (BLK_S, local), 0
        )
        pick = jnp.where(ahead == want * BLK_S, 1.0, 0.0).astype(jnp.bfloat16)
        stk[r - 1] = dot(pick, kt_ref[...], NT).astype(jnp.bfloat16)
        stv[r - 1] = dot(pick, v_ref[...]).astype(jnp.bfloat16)
    bk_ref[(n - 1) * BLK_S:, :] = jnp.zeros((BLK_S, bk_ref.shape[1]), jnp.bfloat16)
    bv_ref[(n - 1) * BLK_S:, :] = jnp.zeros((BLK_S, bv_ref.shape[1]), jnp.bfloat16)
    for r in range(1, n):
        rows = pl.ds((r - 1) * BLK_S, BLK_S)
        rest.append(send(stk.at[r - 1], bk_ref.at[rows], 3, r - 1, ring(r)))
        rest.append(send(stv.at[r - 1], bv_ref.at[rows], 4, r - 1, ring(r)))

    fetch.wait()

    def norm(h, best):
        q = qs[h].astype(jnp.float32)
        return jnp.maximum(best, jnp.sum(q * q, axis=0, keepdims=True))

    best = lax.fori_loop(0, qs.shape[0], norm, jnp.zeros((1, local), jnp.float32))
    qn_ref[...] = jnp.broadcast_to(best, qn_ref.shape)

    for copy in sums:
        copy.wait()
    total = part[head]
    for r in range(1, heads):
        total = total + got[r - 1]
    g_ref[...] = jax.nn.sigmoid(total)
    for copy in rest:
        copy.wait()


def attention_kernel(
    n, segs, hc, local, step_heads,
    sel_ref, q_ref, kt_ref, v_ref, pk_ref, pv_ref, bk_ref, bv_ref, ck_ref, cv_ref, qn_ref, g_ref,
    o_ref,
    kw, vtw, vtp, lw, lp, lc, mixed_ref, flag,
):
    f32, bf16 = jnp.float32, jnp.bfloat16
    me = lax.axis_index("ctx") * segs + lax.axis_index("seg")
    tile = pl.program_id(0)
    sub = pl.program_id(1)
    rows = TILE * step_heads
    span = WINDOW + TILE
    dk = kt_ref.shape[0]
    dv = v_ref.shape[1]
    nc = ck_ref.shape[0]
    npk = (n - 1) * BLK_S
    per = local // BLK_S
    coef = dk ** -0.5

    @pl.when((tile == 0) & (sub == 0))
    def _():
        kw[:WINDOW] = pk_ref[:, local - WINDOW:].astype(f32).T.astype(bf16)
        kw[WINDOW:] = kt_ref[...].astype(f32).T.astype(bf16)
        vtw[:, :WINDOW] = pv_ref[local - WINDOW:, :].astype(f32).T.astype(bf16)
        vtw[:, WINDOW:] = v_ref[...].astype(f32).T.astype(bf16)
        vtp[...] = bv_ref[...].astype(f32).T.astype(bf16)
        lc[:dv] = cv_ref[...].astype(f32).T.astype(bf16)
        lc[dv:] = jnp.where(
            lax.broadcasted_iota(jnp.int32, (16, nc), 0) == 0, 1.0, 0.0
        ).astype(bf16)
        top = jnp.zeros((1, 1), f32)
        for ref in (kw, bk_ref, ck_ref):
            part = ref[...].astype(f32)
            top = jnp.maximum(top, jnp.max(jnp.sum(part * part, axis=1, keepdims=True), axis=0, keepdims=True))
        worst = jnp.max(qn_ref[...]) * jnp.max(top) * (1.02 * coef * coef)
        flag[0] = jnp.where(worst < BOUND * BOUND, 1, 0)

    def chosen(blocks, keep):
        found = jnp.zeros(blocks.shape, jnp.bool_)
        for i in range(NSEL):
            found = found | (blocks == sel_ref[tile, i])
        return found & keep

    def chosen_peer(owner):
        found = jnp.zeros(owner.shape, jnp.bool_)
        for i in range(NSEL):
            entry = sel_ref[tile, i]
            found = found | ((owner * per <= entry) & (entry < owner * per + per))
        return found & (owner >= 0)

    def window_parts(shape, dim):
        pos = me * local + tile * TILE - WINDOW + lax.broadcasted_iota(jnp.int32, shape, dim)
        own = chosen(pos // BLK_S, pos >= me * local)
        return pos >= 0, own

    def peer_part(shape, dim):
        slot = lax.broadcasted_iota(jnp.int32, shape, dim) // BLK_S
        return chosen_peer(me - 1 - slot)

    @pl.when(sub == 0)
    def _():
        valid, own = window_parts((1, span), 1)
        valid, own = valid.astype(f32), own.astype(f32)
        begin = pl.multiple_of(tile * TILE, TILE)
        vt = vtw[:, pl.ds(begin, span)].astype(f32)
        lw[:dv] = (vt * valid).astype(bf16)
        lw[dv:2 * dv] = (vt * own).astype(bf16)
        line = lax.broadcasted_iota(jnp.int32, (16, span), 0)
        lw[2 * dv:] = jnp.where(line == 0, valid, jnp.where(line == 1, own, 0.0)).astype(bf16)
        live = peer_part((1, npk), 1).astype(f32)
        lp[:dv] = (vtp[:, :npk].astype(f32) * live).astype(bf16)
        line = lax.broadcasted_iota(jnp.int32, (16, npk), 0)
        lp[dv:] = jnp.where(line == 0, live, 0.0).astype(bf16)

    q = jnp.concatenate([q_ref[h] for h in range(step_heads)], axis=1)

    def gate(c):
        first = c * hc + sub * step_heads
        return jnp.concatenate([g_ref[pl.ds(first + h, 1), :] for h in range(step_heads)], axis=1)

    gate_c, gate_f, gate_w = gate(0), gate(1), gate(2)
    begin = pl.multiple_of(tile * TILE, TILE)
    keys_w = kw[pl.ds(begin, span), :]
    keys_p = bk_ref[:npk, :]
    safe = flag[0] == 1

    def token(shape):
        return lax.rem(lax.broadcasted_iota(jnp.int32, shape, 1), TILE)

    def coarse_mask():
        shape = (nc, rows)
        end = lax.broadcasted_iota(jnp.int32, shape, 0) * BLK_C + (BLK_C - 1)
        return end <= token(shape) + (me * local + tile * TILE)

    def put(mixed):
        for h in range(step_heads):
            mixed_ref[pl.ds(sub * step_heads + h, TILE, stride=hc), :] = mixed[:, h * TILE:(h + 1) * TILE].T

    @pl.when(safe)
    def _():
        scale = coef * 1.4426950408889634
        ew = jnp.exp2(dot(keys_w, q) * scale)
        key = lax.broadcasted_iota(jnp.int32, (TILE, rows), 0)
        tok = token((TILE, rows))
        low = jnp.where(key > tok, ew[:TILE], 0.0)
        high = jnp.where(key <= tok, ew[WINDOW:], 0.0)
        ew = jnp.concatenate(
            [low.astype(bf16), ew[TILE:WINDOW].astype(bf16), high.astype(bf16)], axis=0
        )
        ow = dot(lw[...], ew)
        ep = jnp.exp2(dot(keys_p, q) * scale).astype(bf16)
        op = dot(lp[...], ep)
        ec = jnp.exp2(dot(ck_ref[...], q) * scale)
        oc = dot(lc[...], jnp.where(coarse_mask(), ec, 0.0).astype(bf16))
        tw = ow[2 * dv:2 * dv + 1]
        tf = ow[2 * dv + 1:2 * dv + 2] + op[dv:dv + 1]
        tc = oc[dv:dv + 1]

        def share(gate, total):
            return jnp.where(total > 0.0, gate / jnp.where(total > 0.0, total, 1.0), 0.0)

        mixed = (
            share(gate_c, tc) * oc[:dv]
            + share(gate_f, tf) * (ow[dv:2 * dv] + op[:dv])
            + share(gate_w, tw) * ow[:dv]
        )
        put(mixed)

    @pl.when(jnp.logical_not(safe))
    def _():
        tok = token((span, rows))
        key = lax.broadcasted_iota(jnp.int32, (span, rows), 0)
        valid, own = window_parts((span, rows), 0)
        causal = key - WINDOW <= tok
        sw = dot(keys_w, q) * coef
        sp = dot(keys_p, q) * coef
        sc = dot(ck_ref[...], q) * coef

        def top(scores, allowed):
            return jnp.max(jnp.where(allowed, scores, -1e30), axis=0, keepdims=True)

        def weigh(scores, allowed, high):
            e = jnp.where(allowed, jnp.exp(jnp.where(allowed, scores - high, 0.0)), 0.0)
            return e.astype(bf16), jnp.sum(e, axis=0, keepdims=True)

        vt = vtw[:, pl.ds(begin, span)]
        ok = valid & causal & (key > tok)
        e, total = weigh(sw, ok, top(sw, ok))
        out_w = dot(vt, e) / jnp.maximum(total, 1.0)
        ok = own & causal
        live = peer_part((npk, rows), 0)
        high = jnp.maximum(top(sw, ok), top(sp, live))
        e, total = weigh(sw, ok, high)
        ep, more = weigh(sp, live, high)
        out_f = (dot(vt, e) + dot(vtp[:, :npk], ep)) / jnp.maximum(total + more, 1.0)
        ok = coarse_mask()
        e, total = weigh(sc, ok, top(sc, ok))
        out_c = dot(lc[:dv], e) / jnp.maximum(total, 1.0)
        mixed = gate_c * out_c + gate_f * out_f + gate_w * out_w
        put(mixed)

    @pl.when(sub == hc // step_heads - 1)
    def _():
        o_ref[...] = mixed_ref[...].astype(bf16)


def on_device(
    n, segs, heads,
    tokens_x, gate_weight, queries, keys, values, comp_key_weight, comp_value_weight, selected,
):
    bf16, f32 = jnp.bfloat16, jnp.float32
    local, hc, dk = queries.shape
    dv = values.shape[2]
    rows_w = gate_weight.shape[0] * gate_weight.shape[1]
    weight = jnp.transpose(gate_weight, (1, 0, 2)).reshape(rows_w, -1)
    share = rows_w // heads
    k2, v2 = keys.reshape(local, dk).T, values.reshape(local, dv)
    chosen = selected.reshape(selected.shape[0], NSEL)
    coarse = local // BLK_C
    vmem = pl.BlockSpec(memory_space=pltpu.VMEM)
    shape = jax.ShapeDtypeStruct
    q3 = jnp.transpose(queries, (1, 2, 0))
    gates, pk, pv, ck, cv, bk, bv, qn = pl.pallas_call(
        functools.partial(exchange_kernel, n, segs, heads),
        out_shape=[
            shape((share, local), f32),
            shape((dk, local), bf16), shape((local, dv), bf16),
            shape((n * coarse, dk), bf16), shape((n * coarse, dv), bf16),
            shape((n * BLK_S, dk), bf16), shape((n * BLK_S, dv), bf16),
            shape((8, local), f32),
        ],
        in_specs=[vmem] * 7 + [pl.BlockSpec(memory_space=pl.ANY)],
        out_specs=[vmem] * 8,
        scratch_shapes=[
            pltpu.VMEM((heads, share, local), f32),
            pltpu.VMEM((heads - 1, share, local), f32),
            pltpu.VMEM((coarse, dk), bf16),
            pltpu.VMEM((coarse, dv), bf16),
            pltpu.VMEM((n - 1,) + chosen.shape, jnp.int32),
            pltpu.VMEM((n - 1, BLK_S, dk), bf16),
            pltpu.VMEM((n - 1, BLK_S, dv), bf16),
            pltpu.VMEM((hc, dk, local), bf16),
            pltpu.SemaphoreType.DMA((6, n)),
            pltpu.SemaphoreType.DMA((6, n)),
            pltpu.SemaphoreType.DMA((heads,)),
            pltpu.SemaphoreType.DMA((heads,)),
            pltpu.SemaphoreType.DMA,
        ],
        compiler_params=pltpu.CompilerParams(collective_id=0, has_side_effects=True),
        name="exchange",
    )(tokens_x, weight, k2, v2, comp_key_weight[0], comp_value_weight[0], chosen, q3)

    rows = TILE * hc
    span = WINDOW + TILE
    npk = (n - 1) * BLK_S
    width = span + npk + n * coarse
    step_heads = hc
    while step_heads > 2 and step_heads * TILE * width > KEY_ROWS:
        step_heads //= 2
    out = pl.pallas_call(
        functools.partial(attention_kernel, n, segs, hc, local, step_heads),
        grid=(local // TILE, hc // step_heads),
        out_shape=shape((local * hc, dv), bf16),
        in_specs=[
            pl.BlockSpec(memory_space=pltpu.SMEM),
            pl.BlockSpec((step_heads, dk, TILE), lambda i, j: (j, 0, i)),
        ] + [vmem] * 9 + [pl.BlockSpec((share, TILE), lambda i, j: (0, i))],
        out_specs=pl.BlockSpec((rows, dv), lambda i, j: (i, 0)),
        scratch_shapes=[
            pltpu.VMEM((WINDOW + local, dk), bf16),
            pltpu.VMEM((dv, WINDOW + local), bf16),
            pltpu.VMEM((dv, n * BLK_S), bf16),
            pltpu.VMEM((2 * dv + 16, span), bf16),
            pltpu.VMEM((dv + 16, npk), bf16),
            pltpu.VMEM((dv + 16, n * coarse), bf16),
            pltpu.VMEM((rows, dv), f32),
            pltpu.SMEM((1,), jnp.int32),
        ],
        compiler_params=pltpu.CompilerParams(
            dimension_semantics=("arbitrary", "arbitrary"), vmem_limit_bytes=60 * 1024 * 1024
        ),
        name="attend",
    )(chosen, q3, k2, v2, pk, pv, bk, bv, ck, cv, qn, gates)
    return out.reshape(local, hc, dv)


def solution(mesh):
    in_specs = (
        P(("ctx", "seg"), "head"),
        P(None, None, "head"),
        P(("ctx", "seg"), "head", None),
        P(("ctx", "seg"), "head", None),
        P(("ctx", "seg"), "head", None),
        P("head", None, None),
        P("head", None, None),
        P(("ctx", "seg"), "head", None),
    )
    n = mesh.shape["ctx"] * mesh.shape["seg"]
    return jax.shard_map(
        functools.partial(on_device, n, mesh.shape["seg"], mesh.shape["head"]),
        mesh=mesh, in_specs=in_specs, out_specs=P(("ctx", "seg"), "head", None), check_vma=False,
    )
```
